512 devices in a mesh: req: 128 (over y, z, core), tp: 4 (over x).
Axes of the slice: x: 4, y: 8, z: 8, core: 2. Of those that a mesh axis runs over, the one named last changes fastest.
Arguments:
- attn_out: bfloat16 [8192, 2048], P('req', 'tp'), may hold values from -6 to 6
- w_out: bfloat16 [2048, 2048], P('tp'), may hold values from -0.125 to 0.125
- residual: bfloat16 [8192, 2048], P('req', 'tp'), may hold values from -6 to 6
- routes: int32 [8192, 6], P('req'), may hold values from 0 to 127, all different within a row; in each aligned block of 64 rows (0 to 63, 64 to 127, ...) at most 6 rows name the same one
- gates: float32 [8192, 6], P('req'), may hold values from 0.05 to 1
- w_gate: bfloat16 [128, 2048, 1024], P('req', None, 'tp'), as said below
- w_up: bfloat16 [128, 2048, 1024], P('req', None, 'tp'), as said below
- w_down: bfloat16 [128, 1024, 2048], P('req', None, 'tp'), as said below
- norm_gain: float32 [2048], P('tp'), may hold values from 0.1 to 1.9
Outputs:
- normed: bfloat16 [8192, 2048], P('req', 'tp')
The draws below stay inside these ranges and needn't reach their ends.
Inputs may be any that keep to these rules, and one draw needn't show every extreme that they name: `routes`: each row names 6 different slots. In the 64 rows of one index of req no slot is named by more than 6 rows, a bound that some block reaches. `w_gate`: slots 2 e and 2 e + 1 hold the same expert e: their weights are equal. `w_up`: slots 2 e and 2 e + 1 hold the same expert e: their weights are equal. `w_down`: slots 2 e and 2 e + 1 hold the same expert e: their weights are equal.
All inputs are finite; a program needn't handle non-finite values.
Results may differ from the reference program's by a relative error of at most 0.0056.
Values may be sent and summed in bfloat16 or wider, within the bound.
A program may use at most 64 MiB of HBM per device.

```python
import math
import jax
import jax.numpy as jnp
import numpy as np
from jax import lax

D = 2048
HID = 1024
TOPK = 6
ROWS = 64
TOKENS = 8192
CAP = 6
N_REQ = 128


def expert_table(key, fan_in, width, salt):
    per_expert = jax.random.normal(jax.random.fold_in(key, salt), (N_REQ // 2, fan_in, width), jnp.float32)
    per_expert = per_expert * fan_in ** (-0.5)
    return jnp.repeat(per_expert, 2, axis=0)


def draw_w_gate(key, part):
    return expert_table(key, D, HID, 11).astype(jnp.bfloat16)


def draw_w_up(key, part):
    return expert_table(key, D, HID, 23).astype(jnp.bfloat16)


def draw_w_down(key, part):
    return expert_table(key, HID, D, 37).astype(jnp.bfloat16)


def steps_of(key, dims, pieces, smallest, largest):
    def one(dim, blocks):
        steps = jax.random.uniform(jax.random.fold_in(jax.random.fold_in(key, 6), dim), (blocks,), jnp.float32, smallest / len(pieces), largest / len(pieces))
        return jnp.repeat(jnp.exp(steps), dims[dim] // blocks).reshape((-1,) + (1,) * (len(dims) - dim - 1))

    factor_of = one(*pieces[0])
    for cut in pieces[1:]:
        factor_of = factor_of * one(*cut)
    return factor_of


def routed_block(key, own, number, rows, number_of, top, reach, slope):
    sequence = jax.random.permutation(key, number_of)
    crowded, usual = portions_of(number_of, rows * top, reach, slope, True), portions_of(number_of, rows * top, reach, slope, False)
    places = jnp.arange(number_of)

    def named(lengths, offset_by):
        used = int((lengths > 0).sum())
        fixed = max(1, used // 4)
        moved = fixed + (places - fixed + offset_by * (used - fixed)) % max(1, number_of - fixed)
        return jnp.zeros((number_of,), jnp.int32).at[sequence[jnp.where(places < fixed, places, moved)]].set(jnp.asarray(lengths, jnp.int32))

    lengths = jnp.where(number % 4 == 0, named(crowded, number // 4), named(usual, number - number // 4 - 1))
    mixed = jax.random.permutation(jax.random.fold_in(own, 3), number_of)
    donor, receiver = mixed[0:number_of // 2 * 2:2], mixed[1:number_of // 2 * 2:2]
    margin = jnp.minimum(lengths[donor] - 1, reach - lengths[receiver]) // 2
    margin = jnp.where((donor == sequence[0]) | (receiver == sequence[0]) | (lengths[receiver] == 0), 0, jnp.maximum(margin, 0))
    moved = jax.random.randint(jax.random.fold_in(own, 4), (number_of // 2,), 0, 1 << 20) % (margin + 1)
    lengths = lengths.at[donor].add(-moved).at[receiver].add(moved)
    members = jnp.searchsorted(jnp.cumsum(lengths), jnp.arange(rows * top), side="right").astype(jnp.int32)
    listing = members.reshape(top, rows).T
    listing = listing[jax.random.permutation(jax.random.fold_in(own, 1), rows)]
    offset_by = jax.random.randint(jax.random.fold_in(own, 2), (rows, 1), 0, top)
    return jnp.take_along_axis(listing, (jnp.arange(top)[None, :] + offset_by) % top, axis=1)


def portions_of(number_of, total, most, slope, full):
    loads = [(1 << 20) // math.isqrt(rank ** slope) + 1 for rank in range(1, number_of + 1)]
    largest = most if full else min(most, max(-(-total // number_of), total * loads[0] // sum(loads)))
    least = 1 if total - largest >= number_of - 1 else 0
    given, rest = [largest] + [least] * (number_of - 1), total - largest - least * (number_of - 1)
    while rest > 0:
        free = [i for i in range(1, number_of) if given[i] < largest] or [i for i in range(1, number_of) if given[i] < most]
        mass, left = sum([loads[i] for i in free]), rest
        for i in free:
            extra = min(most - given[i], max(1, left * loads[i] // mass), rest)
            given[i] = given[i] + extra
            rest = rest - extra
    return np.array(given)


def gaussian(key, dims, deviation, most, cuts=(), kind=jnp.bfloat16):
    level = steps_of(key, dims, cuts, -0.22, 0.18) if cuts else 1.0
    array = jax.random.normal(key, dims, jnp.float32) * deviation * level
    return jnp.minimum(jnp.maximum(array, -most), most).astype(kind)


def setup_inputs(seed: int = 0) -> dict:
    key_list = jax.random.split(jax.random.key(seed), 10)
    attn_out = gaussian(key_list[0], (TOKENS, D), 1.0, 6.0, ((0, 128), (1, 4)))
    w_out = gaussian(key_list[1], (D, D), D ** -0.5, 0.125, ((0, 4),))
    residual = gaussian(key_list[2], (TOKENS, D), 1.0, 6.0, ((0, 128), (1, 4)))
    routes_keys = jax.random.split(jax.random.fold_in(key_list[3], 1), TOKENS // ROWS)
    routes_turns = jax.random.permutation(jax.random.fold_in(key_list[3], 3), TOKENS // ROWS)
    routes = jax.vmap(lambda own, number: routed_block(jax.random.fold_in(key_list[3], 2), own, number, ROWS, N_REQ, TOPK, CAP, 2))(routes_keys, routes_turns).reshape((TOKENS, TOPK))
    gates = jnp.clip(jnp.exp(math.log(1.0) - 2.9957323 * jax.random.uniform(key_list[4], (TOKENS, TOPK), jnp.float32) ** steps_of(key_list[4], (TOKENS, TOPK), ((0, 128),), -0.2, 0.2)), 0.05, 1.0)
    w_gate = draw_w_gate(jax.random.fold_in(key_list[9], 71), 0)
    w_up = draw_w_up(jax.random.fold_in(key_list[9], 71), 0)
    w_down = draw_w_down(jax.random.fold_in(key_list[9], 71), 0)
    norm_gain = jnp.clip(1.0 + 0.18 * jax.random.normal(key_list[8], (D,), jnp.float32), 0.1, 1.9)
    return {"attn_out": attn_out, "w_out": w_out, "residual": residual, "routes": routes, "gates": gates, "w_gate": w_gate, "w_up": w_up, "w_down": w_down, "norm_gain": norm_gain}


def reference(attn_out, w_out, residual, routes, gates, w_gate, w_up, w_down, norm_gain):
    projected = residual.astype(jnp.float32) + jnp.dot(attn_out, w_out, preferred_element_type=jnp.float32)
    sent = projected.astype(jnp.bfloat16)
    per_block = routes.reshape(N_REQ, ROWS * TOPK)
    one_hot = (per_block[:, :, None] == jnp.arange(N_REQ, dtype=jnp.int32)[None, None, :]).astype(jnp.int32)
    position = lax.optimization_barrier(jnp.sum(one_hot * (jnp.cumsum(one_hot, axis=1) - 1), axis=2))
    block_ids = jnp.arange(N_REQ, dtype=jnp.int32)[:, None]
    global_index = (per_block * (N_REQ * CAP) + block_ids * CAP + position).reshape(-1).astype(jnp.int32)
    token_ids = jnp.repeat(jnp.arange(TOKENS, dtype=jnp.int32), TOPK)
    source_table = jnp.zeros((N_REQ * N_REQ * CAP,), jnp.int32).at[global_index].set(token_ids)
    weight_table = jnp.zeros((N_REQ * N_REQ * CAP,), jnp.float32).at[global_index].set(gates.reshape(-1))
    source_table = source_table.reshape(N_REQ, N_REQ * CAP)
    weight_table = weight_table.reshape(N_REQ, N_REQ * CAP)

    def one_slot(running, items):
        gate_w, up_w, down_w, sources, weights = items
        expert_rows = sent[sources]
        gate_act = jnp.dot(expert_rows, gate_w, preferred_element_type=jnp.float32)
        up_act = jnp.dot(expert_rows, up_w, preferred_element_type=jnp.float32)
        hidden = (jax.nn.silu(gate_act) * up_act).astype(jnp.bfloat16)
        expert_out = jnp.dot(hidden, down_w, preferred_element_type=jnp.float32).astype(jnp.bfloat16)
        running = running.at[sources].add(weights[:, None] * expert_out.astype(jnp.float32))
        return (running, None)
    start = jnp.zeros((TOKENS, D), jnp.float32)
    routed_sum, unused = lax.scan(one_slot, start, (w_gate, w_up, w_down, source_table, weight_table))
    combined = projected + routed_sum
    mean_square = lax.optimization_barrier(jnp.mean(combined * combined, axis=1, keepdims=True))
    return (combined * lax.rsqrt(mean_square + 1e-06) * norm_gain[None, :]).astype(jnp.bfloat16)
```

```python
import functools

import jax
import jax.numpy as jnp
from jax import lax
from jax.experimental import pallas as pl
from jax.experimental.pallas import tpu as pltpu
from jax.sharding import PartitionSpec as P

NY, NZ, NC, NX = 8, 8, 2, 4
CAP = 6
PAIR = NC * CAP
F32, BF16 = jnp.float32, jnp.bfloat16
MESH = pl.DeviceIdType.MESH


def dot(a, b):
    return jnp.dot(a, b, preferred_element_type=F32)


def dot_rows(a, b):
    return lax.dot_general(a, b, (((0,), (0,)), ((), ())), preferred_element_type=F32)


def step_of(k):
    return (2 * (k % 2) - 1) * ((k + 1) // 2)


def kernel(
    attn, w_out, resid, meta, w_gate, w_up, w_down, gain, out,
    wo, wgu, wd, part, part32, rs_in, proj, meta_all, pick, comb_hi, comb_lo,
    rows, zsend, feat, hid, oexp, back, acc, ysend, yin, ss_own, ss_in,
    load_sem, meta_s, meta_r, rs_s, rs_r, yag_s, yag_r, z_s, z_r,
    xa_s, xa_r, xf_s, xf_r, ha_s, ha_r, hf_s, hf_r, b_s, b_r, yr_s, yr_r, ss_s, ss_r,
):
    nrow, width = attn.shape
    full = w_out.shape[1]
    chunk = NY * PAIR
    half = chunk // 2
    hw = w_gate.shape[1]
    req, x = lax.axis_index("req"), lax.axis_index("tp")
    c = req % NC
    z = (req // NC) % NZ
    y = req // (NC * NZ)

    def at_x(d):
        return {"tp": (x + d + NX) % NX}

    def at_y(d):
        return {"req": (((y + d + NY) % NY) * NZ + z) * NC + c}

    def at_z(d):
        return {"req": (y * NZ + (z + d + NZ) % NZ) * NC + c}

    def remote(src, dst, s, r, dev):
        return pltpu.make_async_remote_copy(
            src_ref=src, dst_ref=dst, send_sem=s, recv_sem=r, device_id=dev, device_id_type=MESH
        )

    loads = [
        pltpu.make_async_copy(w_out, wo, load_sem.at[0]),
        pltpu.make_async_copy(w_gate, wgu.at[:, :hw], load_sem.at[1]),
        pltpu.make_async_copy(w_up, wgu.at[:, hw:], load_sem.at[2]),
        pltpu.make_async_copy(w_down, wd, load_sem.at[3]),
    ]
    for load in loads:
        load.start()

    barrier = pltpu.get_barrier_semaphore()
    partners = [at_x(d) for d in range(1, NX)]
    partners += [at_y(d) for d in range(1, NY)]
    partners += [at_z(d) for d in range(1, NZ)]
    for dev in partners:
        pl.semaphore_signal(barrier, inc=1, device_id=dev, device_id_type=MESH)

    loads[0].wait()
    for q in range(NX):
        value = dot(attn[...], wo[:, q * width:(q + 1) * width])
        part32[q] = value
        part[q] = value.astype(BF16)
    meta_all[y] = meta[...]
    pl.semaphore_wait(barrier, len(partners))

    meta_copies, rs_copies = [], []
    for d in range(1, NY):
        copy = remote(meta, meta_all.at[y], meta_s.at[d - 1], meta_r.at[d - 1], at_y(d))
        copy.start()
        meta_copies.append(copy)
    for d in range(1, NX):
        copy = remote(part.at[(x + d) % NX], rs_in.at[d - 1], rs_s.at[d - 1], rs_r.at[d - 1], at_x(d))
        copy.start()
        rs_copies.append(copy)

    for d in range(1, NY):
        remote(
            meta, meta_all.at[(y - d + NY) % NY], meta_s.at[d - 1], meta_r.at[d - 1], at_y(d)
        ).wait_recv()
    lanes = 2 * nrow
    place = lax.broadcasted_iota(jnp.int32, (chunk, lanes), 0)
    lane = lax.broadcasted_iota(jnp.int32, (chunk, lanes), 1)
    place_y, place_c, place_p = place // PAIR, (place // CAP) % NC, place % CAP
    before = lax.broadcasted_iota(jnp.int32, (lanes, lanes), 0)
    after = lax.broadcasted_iota(jnp.int32, (lanes, lanes), 1)
    earlier = ((before < after) & (before // nrow == after // nrow)).astype(F32).astype(BF16)

    def plan(zz, carry):
        slot = ((y * NZ + zz) * NC + place_c).astype(F32)
        for j in range(NY // 2):
            both = meta_all[2 * j] + meta_all[2 * j + 1]
            mine = place_y == 2 * j + lane // nrow
            hit = jnp.zeros((chunk, lanes), F32)
            gate = jnp.zeros((chunk, lanes), F32)
            for k in range(6):
                same = mine & (both[k:k + 1, :] == slot)
                hit = jnp.where(same, 1.0, hit)
                gate = jnp.where(same, both[8 + k:9 + k, :], gate)
            rank = dot(hit.astype(BF16), earlier)
            chosen = (hit > 0.0) & (rank == place_p.astype(F32))
            here = pl.ds(j * lanes, lanes)
            pick[zz, :, here] = jnp.where(chosen, 1.0, 0.0).astype(BF16)
            gate = jnp.where(chosen, gate, 0.0)
            high = gate.astype(BF16)
            comb_hi[zz, :, here] = high
            comb_lo[zz, :, here] = (gate - high.astype(F32)).astype(BF16)
        return carry

    lax.fori_loop(0, NZ, plan, 0)

    own = part32[x] + resid[...].astype(F32)
    for d in range(1, NX):
        remote(part.at[0], rs_in.at[d - 1], rs_s.at[d - 1], rs_r.at[d - 1], at_x(d)).wait_recv()
        own = own + rs_in[d - 1].astype(F32)
    proj[...] = own
    rows[y] = own.astype(BF16)

    yag = []
    for s in range(1, NY // 2 + 1):
        cut = s == NY // 2
        right = rows.at[(y - s + 1 + NY) % NY]
        left = rows.at[(y + s - 1) % NY]
        if s > 1:
            remote(right, right, yag_s.at[0, s - 2], yag_r.at[0, s - 2], at_y(-1)).wait_recv()
            remote(left, left, yag_s.at[1, s - 2], yag_r.at[1, s - 2], at_y(1)).wait_recv()
        if cut:
            right, left = right.at[:nrow // 2], left.at[nrow // 2:]
        one = remote(right, right, yag_s.at[0, s - 1], yag_r.at[0, s - 1], at_y(1))
        two = remote(left, left, yag_s.at[1, s - 1], yag_r.at[1, s - 1], at_y(-1))
        one.start()
        two.start()
        yag += [one, two]
    far = rows.at[(y + NY // 2) % NY]
    remote(far.at[:nrow // 2], far.at[:nrow // 2], yag_s.at[0, NY // 2 - 1], yag_r.at[0, NY // 2 - 1], at_y(-1)).wait_recv()
    remote(far.at[nrow // 2:], far.at[nrow // 2:], yag_s.at[1, NY // 2 - 1], yag_r.at[1, NY // 2 - 1], at_y(1)).wait_recv()

    def source_of(k):
        return (z - step_of(k) + NZ) % NZ

    def xa(k, right):
        block = feat.at[x, source_of(k)]
        i = 0 if right else 1
        return remote(block, block, xa_s.at[k, i], xa_r.at[k, i], at_x(1 if right else -1))

    def xf(k, right):
        n = source_of(k)
        i = 0 if right else 1
        rng = pl.ds(0, half) if right else pl.ds(half, half)
        block = feat.at[(x + NX - 1) % NX if right else (x + 1) % NX, n, rng]
        return remote(block, block, xf_s.at[k, i], xf_r.at[k, i], at_x(1 if right else -1))

    def ha(k, right):
        block = hid.at[x, source_of(k)]
        i = 0 if right else 1
        return remote(block, block, ha_s.at[k, i], ha_r.at[k, i], at_x(1 if right else -1))

    def hf(k, right):
        n = source_of(k)
        i = 0 if right else 1
        rng = pl.ds(0, half) if right else pl.ds(half, half)
        block = hid.at[(x + NX - 1) % NX if right else (x + 1) % NX, n, rng]
        return remote(block, block, hf_s.at[k, i], hf_r.at[k, i], at_x(1 if right else -1))

    def zsend_copy(k):
        n = (z + step_of(k) + NZ) % NZ
        return remote(zsend.at[n], feat.at[x, z], z_s.at[k], z_r.at[k], at_z(step_of(k)))

    def zback_copy(k):
        n = source_of(k)
        return remote(oexp.at[n], back.at[z], b_s.at[k], b_r.at[k], at_z(-step_of(k)))

    all_rows = rows[...].reshape(NY * nrow, width)
    feat[x, z] = dot(pick[z], all_rows).astype(BF16)
    xa(0, True).start()
    xa(0, False).start()

    def scatter(k, carry):
        n = (z + step_of(k) + NZ) % NZ
        zsend[n] = dot(pick[n], rows[...].reshape(NY * nrow, width)).astype(BF16)
        zsend_copy(k).start()
        return carry

    lax.fori_loop(1, NZ, scatter, 0)
    for load in loads[1:]:
        load.wait()

    def stage(i, carry):
        @pl.when((i >= 1) & (i < NZ))
        def _():
            n = source_of(i)
            remote(zsend.at[n], feat.at[x, n], z_s.at[i], z_r.at[i], at_z(step_of(i))).wait_recv()
            xa(i, True).start()
            xa(i, False).start()

        @pl.when((i >= 1) & (i < NZ + 1))
        def _():
            k = i - 1
            n = source_of(k)
            left, right = feat.at[(x + NX - 1) % NX, n], feat.at[(x + 1) % NX, n]
            remote(left, left, xa_s.at[k, 0], xa_r.at[k, 0], at_x(-1)).wait_recv()
            xf(k, True).start()
            remote(right, right, xa_s.at[k, 1], xa_r.at[k, 1], at_x(1)).wait_recv()
            xf(k, False).start()

        @pl.when((i >= 2) & (i < NZ + 2))
        def _():
            k = i - 2
            n = source_of(k)
            far = feat.at[(x + 2) % NX, n]
            low, high = far.at[pl.ds(0, half)], far.at[pl.ds(half, half)]
            remote(low, low, xf_s.at[k, 0], xf_r.at[k, 0], at_x(-1)).wait_recv()
            remote(high, high, xf_s.at[k, 1], xf_r.at[k, 1], at_x(1)).wait_recv()
            both = dot(feat[0, n], wgu[0:width, :])
            for q in range(1, NX):
                both = both + dot(feat[q, n], wgu[q * width:(q + 1) * width, :])
            gate, up = both[:, :hw], both[:, hw:]
            hid[x, n] = (gate / (1.0 + jnp.exp(-gate)) * up).astype(BF16)
            ha(k, True).start()
            ha(k, False).start()

        @pl.when((i >= 3) & (i < NZ + 3))
        def _():
            k = i - 3
            n = source_of(k)
            left, right = hid.at[(x + NX - 1) % NX, n], hid.at[(x + 1) % NX, n]
            remote(left, left, ha_s.at[k, 0], ha_r.at[k, 0], at_x(-1)).wait_recv()
            hf(k, True).start()
            remote(right, right, ha_s.at[k, 1], ha_r.at[k, 1], at_x(1)).wait_recv()
            hf(k, False).start()

        @pl.when(i >= 4)
        def _():
            k = i - 4
            n = source_of(k)
            far = hid.at[(x + 2) % NX, n]
            low, high = far.at[pl.ds(0, half)], far.at[pl.ds(half, half)]
            remote(low, low, hf_s.at[k, 0], hf_r.at[k, 0], at_x(-1)).wait_recv()
            remote(high, high, hf_s.at[k, 1], hf_r.at[k, 1], at_x(1)).wait_recv()
            value = dot(hid[0, n], wd[0:hw, :])
            for q in range(1, NX):
                value = value + dot(hid[q, n], wd[q * hw:(q + 1) * hw, :])

            @pl.when(k == 0)
            def _():
                back[z] = value.astype(BF16)

            @pl.when(k > 0)
            def _():
                oexp[n] = value.astype(BF16)
                zback_copy(k).start()

        return carry

    lax.fori_loop(0, NZ + 4, stage, 0)

    def gather(k, carry):
        n = (z + step_of(k) + NZ) % NZ

        @pl.when(k > 0)
        def _():
            remote(oexp.at[n], back.at[n], b_s.at[k], b_r.at[k], at_z(step_of(k))).wait_recv()

        value = dot_rows(comb_hi[n], back[n]) + dot_rows(comb_lo[n], back[n])

        @pl.when(k == 0)
        def _():
            acc[...] = value

        @pl.when(k > 0)
        def _():
            acc[...] += value

        return carry

    lax.fori_loop(0, NZ, gather, 0)
    for q in range(NY):
        ysend[q] = acc[q * nrow:(q + 1) * nrow, :].astype(BF16)
    yr = []
    for d in (4, 3, 5, 2, 6, 1, 7):
        copy = remote(ysend.at[(y + d) % NY], yin.at[d - 1], yr_s.at[d - 1], yr_r.at[d - 1], at_y(d))
        copy.start()
        yr.append(copy)
    total = proj[...] + acc[pl.ds(pl.multiple_of(y * nrow, nrow), nrow), :]
    for d in range(1, NY):
        remote(ysend.at[0], yin.at[d - 1], yr_s.at[d - 1], yr_r.at[d - 1], at_y(d)).wait_recv()
        total = total + yin[d - 1].astype(F32)

    square = jnp.sum(total * total, axis=1, keepdims=True)
    ss_own[...] = jnp.broadcast_to(square, ss_own.shape)
    ss = []
    for d in range(1, NX):
        copy = remote(ss_own, ss_in.at[d - 1], ss_s.at[d - 1], ss_r.at[d - 1], at_x(d))
        copy.start()
        ss.append(copy)
    for d in range(1, NX):
        remote(ss_own, ss_in.at[d - 1], ss_s.at[d - 1], ss_r.at[d - 1], at_x(d)).wait_recv()
        square = square + ss_in[d - 1][:, 0:1]
    scale = lax.rsqrt(square / full + 1e-06)
    out[...] = (total * scale * gain[...]).astype(BF16)

    for copy in meta_copies + rs_copies + yag + yr + ss:
        copy.wait_send()

    def drain(k, carry):
        for make in (xa, xf, ha, hf):
            make(k, True).wait_send()
            make(k, False).wait_send()

        @pl.when(k > 0)
        def _():
            zsend_copy(k).wait_send()
            zback_copy(k).wait_send()

        return carry

    lax.fori_loop(0, NZ, drain, 0)


def body(attn_out, w_out, residual, routes, gates, w_gate, w_up, w_down, norm_gain):
    nrow, width = attn_out.shape
    full = w_out.shape[1]
    topk = routes.shape[1]
    hw = w_gate.shape[2]
    chunk = NY * PAIR
    y = lax.axis_index("req") // (NC * NZ)
    pad = ((0, 8 - topk), (0, 0))
    tile = jnp.concatenate(
        [jnp.pad(routes.T.astype(F32), pad), jnp.pad(gates.T.astype(F32), pad)], axis=0
    )
    odd = y % 2 == 1
    meta = jnp.concatenate([jnp.where(odd, 0.0, tile), jnp.where(odd, tile, 0.0)], axis=1)
    vmem = pl.BlockSpec(memory_space=pltpu.VMEM)
    anyw = pl.BlockSpec(memory_space=pl.ANY)
    dma = pltpu.SemaphoreType.DMA
    scratch = [
        pltpu.VMEM((width, full), BF16),
        pltpu.VMEM((full, 2 * hw), BF16),
        pltpu.VMEM((NX * hw, width), BF16),
        pltpu.VMEM((NX, nrow, width), BF16),
        pltpu.VMEM((NX, nrow, width), F32),
        pltpu.VMEM((NX - 1, nrow, width), BF16),
        pltpu.VMEM((nrow, width), F32),
        pltpu.VMEM((NY, 16, 2 * nrow), F32),
        pltpu.VMEM((NZ, chunk, NY * nrow), BF16),
        pltpu.VMEM((NZ, chunk, NY * nrow), BF16),
        pltpu.VMEM((NZ, chunk, NY * nrow), BF16),
        pltpu.VMEM((NY, nrow, width), BF16),
        pltpu.VMEM((NZ, chunk, width), BF16),
        pltpu.VMEM((NX, NZ, chunk, width), BF16),
        pltpu.VMEM((NX, NZ, chunk, hw), BF16),
        pltpu.VMEM((NZ, chunk, width), BF16),
        pltpu.VMEM((NZ, chunk, width), BF16),
        pltpu.VMEM((NY * nrow, width), F32),
        pltpu.VMEM((NY, nrow, width), BF16),
        pltpu.VMEM((NY - 1, nrow, width), BF16),
        pltpu.VMEM((nrow, 128), F32),
        pltpu.VMEM((NX - 1, nrow, 128), F32),
        dma((4,)),
        dma((NY - 1,)), dma((NY - 1,)),
        dma((NX - 1,)), dma((NX - 1,)),
        dma((2, NY // 2)), dma((2, NY // 2)),
        dma((NZ,)), dma((NZ,)),
        dma((NZ, 2)), dma((NZ, 2)),
        dma((NZ, 2)), dma((NZ, 2)),
        dma((NZ, 2)), dma((NZ, 2)),
        dma((NZ, 2)), dma((NZ, 2)),
        dma((NZ,)), dma((NZ,)),
        dma((NY - 1,)), dma((NY - 1,)),
        dma((NX - 1,)), dma((NX - 1,)),
    ]
    return pl.pallas_call(
        kernel,
        out_shape=jax.ShapeDtypeStruct((nrow, width), BF16),
        in_specs=[vmem, anyw, vmem, vmem, anyw, anyw, anyw, vmem],
        out_specs=vmem,
        scratch_shapes=scratch,
        compiler_params=pltpu.CompilerParams(collective_id=0, has_side_effects=True),
    )(attn_out, w_out, residual, meta, w_gate[0], w_up[0], w_down[0], norm_gain[None, :])


def solution(mesh):
    placed = (
        P("req", "tp"),
        P("tp", None),
        P("req", "tp"),
        P("req", None),
        P("req", None),
        P("req", None, "tp"),
        P("req", None, "tp"),
        P("req", None, "tp"),
        P("tp"),
    )
    return jax.shard_map(
        body, mesh=mesh, in_specs=placed, out_specs=P("req", "tp"), check_vma=False
    )
```

```python
import functools

import jax
import jax.numpy as jnp
from jax import lax
from jax.experimental import pallas as pl
from jax.experimental.pallas import tpu as pltpu
from jax.sharding import PartitionSpec as P

NY, NZ, NC, NX = 8, 8, 2, 4
CAP = 6
PAIR = NC * CAP
F32, BF16 = jnp.float32, jnp.bfloat16
MESH = pl.DeviceIdType.MESH


def dot(a, b):
    return jnp.dot(a, b, preferred_element_type=F32)


def dot_rows(a, b):
    return lax.dot_general(a, b, (((0,), (0,)), ((), ())), preferred_element_type=F32)


def step_of(k):
    return (2 * (k % 2) - 1) * ((k + 1) // 2)


def kernel(
    attn, w_out, resid, meta, w_gate, w_up, w_down, gain, out,
    wo, wgu, wd, part, part32, rs_in, proj, meta_all, pick, comb_hi, comb_lo,
    rows, zsend, feat, hid, oexp, back, acc, ysend, yin, ss_own, ss_in,
    load_sem, meta_s, meta_r, rs_s, rs_r, yag_s, yag_r, z_s, z_r,
    xa_s, xa_r, xf_s, xf_r, ha_s, ha_r, hf_s, hf_r, b_s, b_r, yr_s, yr_r, ss_s, ss_r,
):
    nrow, width = attn.shape
    full = w_out.shape[1]
    chunk = NY * PAIR
    half = chunk // 2
    hw = w_gate.shape[1]
    req, x = lax.axis_index("req"), lax.axis_index("tp")
    c = req % NC
    pz = (req // NC) % NZ
    py = req // (NC * NZ)
    y = py + c * (pz - py)
    z = pz + c * (py - pz)

    def at_x(d):
        return {"tp": (x + d + NX) % NX}

    def chip(yy, zz):
        return yy * (NZ + c * (1 - NZ)) + zz * (1 + c * (NZ - 1))

    def at_y(d):
        return {"req": chip((y + d + NY) % NY, z) * NC + c}

    def at_z(d):
        return {"req": chip(y, (z + d + NZ) % NZ) * NC + c}

    def remote(src, dst, s, r, dev):
        return pltpu.make_async_remote_copy(
            src_ref=src, dst_ref=dst, send_sem=s, recv_sem=r, device_id=dev, device_id_type=MESH
        )

    loads = [
        pltpu.make_async_copy(w_out, wo, load_sem.at[0]),
        pltpu.make_async_copy(w_gate, wgu.at[:, :hw], load_sem.at[1]),
        pltpu.make_async_copy(w_up, wgu.at[:, hw:], load_sem.at[2]),
        pltpu.make_async_copy(w_down, wd, load_sem.at[3]),
    ]
    for load in loads:
        load.start()

    barrier = pltpu.get_barrier_semaphore()
    partners = [at_x(d) for d in range(1, NX)]
    partners += [at_y(d) for d in range(1, NY)]
    partners += [at_z(d) for d in range(1, NZ)]
    for dev in partners:
        pl.semaphore_signal(barrier, inc=1, device_id=dev, device_id_type=MESH)

    loads[0].wait()
    for q in range(NX):
        value = dot(attn[...], wo[:, q * width:(q + 1) * width])
        part32[q] = value
        part[q] = value.astype(BF16)
    meta_all[y] = meta[...]
    pl.semaphore_wait(barrier, len(partners))

    meta_copies, rs_copies = [], []
    for d in range(1, NY):
        copy = remote(meta, meta_all.at[y], meta_s.at[d - 1], meta_r.at[d - 1], at_y(d))
        copy.start()
        meta_copies.append(copy)
    for d in range(1, NX):
        copy = remote(part.at[(x + d) % NX], rs_in.at[d - 1], rs_s.at[d - 1], rs_r.at[d - 1], at_x(d))
        copy.start()
        rs_copies.append(copy)

    for d in range(1, NY):
        remote(
            meta, meta_all.at[(y - d + NY) % NY], meta_s.at[d - 1], meta_r.at[d - 1], at_y(d)
        ).wait_recv()
    lanes = 2 * nrow
    place = lax.broadcasted_iota(jnp.int32, (chunk, lanes), 0)
    lane = lax.broadcasted_iota(jnp.int32, (chunk, lanes), 1)
    place_y, place_c, place_p = place // PAIR, (place // CAP) % NC, place % CAP
    before = lax.broadcasted_iota(jnp.int32, (lanes, lanes), 0)
    after = lax.broadcasted_iota(jnp.int32, (lanes, lanes), 1)
    earlier = ((before < after) & (before // nrow == after // nrow)).astype(F32).astype(BF16)

    def plan(zz, carry):
        slot = (chip(y, zz) * NC + place_c).astype(F32)
        for j in range(NY // 2):
            both = meta_all[2 * j] + meta_all[2 * j + 1]
            mine = place_y == 2 * j + lane // nrow
            hit = jnp.zeros((chunk, lanes), F32)
            gate = jnp.zeros((chunk, lanes), F32)
            for k in range(6):
                same = mine & (both[k:k + 1, :] == slot)
                hit = jnp.where(same, 1.0, hit)
                gate = jnp.where(same, both[8 + k:9 + k, :], gate)
            rank = dot(hit.astype(BF16), earlier)
            chosen = (hit > 0.0) & (rank == place_p.astype(F32))
            here = pl.ds(j * lanes, lanes)
            pick[zz, :, here] = jnp.where(chosen, 1.0, 0.0).astype(BF16)
            gate = jnp.where(chosen, gate, 0.0)
            high = gate.astype(BF16)
            comb_hi[zz, :, here] = high
            comb_lo[zz, :, here] = (gate - high.astype(F32)).astype(BF16)
        return carry

    lax.fori_loop(0, NZ, plan, 0)

    own = part32[x] + resid[...].astype(F32)
    for d in range(1, NX):
        remote(part.at[0], rs_in.at[d - 1], rs_s.at[d - 1], rs_r.at[d - 1], at_x(d)).wait_recv()
        own = own + rs_in[d - 1].astype(F32)
    proj[...] = own
    rows[y] = own.astype(BF16)

    yag = []
    for d in (4, 3, 5, 2, 6, 1, 7):
        copy = remote(rows.at[y], rows.at[y], yag_s.at[d - 1], yag_r.at[d - 1], at_y(d))
        copy.start()
        yag.append(copy)
    for d in (1, 7, 2, 6, 3, 5, 4):
        block = rows.at[(y - d + NY) % NY]
        remote(block, block, yag_s.at[d - 1], yag_r.at[d - 1], at_y(-d)).wait_recv()

    def source_of(k):
        return (z - step_of(k) + NZ) % NZ

    def xa(k, right):
        block = feat.at[x, source_of(k)]
        i = 0 if right else 1
        return remote(block, block, xa_s.at[k, i], xa_r.at[k, i], at_x(1 if right else -1))

    def xf(k, right):
        n = source_of(k)
        i = 0 if right else 1
        rng = pl.ds(0, half) if right else pl.ds(half, half)
        block = feat.at[(x + NX - 1) % NX if right else (x + 1) % NX, n, rng]
        return remote(block, block, xf_s.at[k, i], xf_r.at[k, i], at_x(1 if right else -1))

    def ha(k, right):
        block = hid.at[x, source_of(k)]
        i = 0 if right else 1
        return remote(block, block, ha_s.at[k, i], ha_r.at[k, i], at_x(1 if right else -1))

    def hf(k, right):
        n = source_of(k)
        i = 0 if right else 1
        rng = pl.ds(0, half) if right else pl.ds(half, half)
        block = hid.at[(x + NX - 1) % NX if right else (x + 1) % NX, n, rng]
        return remote(block, block, hf_s.at[k, i], hf_r.at[k, i], at_x(1 if right else -1))

    def zsend_copy(k):
        n = (z + step_of(k) + NZ) % NZ
        return remote(zsend.at[n], feat.at[x, z], z_s.at[k], z_r.at[k], at_z(step_of(k)))

    def zback_copy(k):
        n = source_of(k)
        return remote(oexp.at[n], back.at[z], b_s.at[k], b_r.at[k], at_z(-step_of(k)))

    all_rows = rows[...].reshape(NY * nrow, width)
    feat[x, z] = dot(pick[z], all_rows).astype(BF16)
    xa(0, True).start()
    xa(0, False).start()

    def scatter(k, carry):
        n = (z + step_of(k) + NZ) % NZ
        zsend[n] = dot(pick[n], rows[...].reshape(NY * nrow, width)).astype(BF16)
        zsend_copy(k).start()
        return carry

    lax.fori_loop(1, NZ, scatter, 0)
    for load in loads[1:]:
        load.wait()

    def stage(i, carry):
        @pl.when((i >= 1) & (i < NZ))
        def _():
            n = source_of(i)
            remote(zsend.at[n], feat.at[x, n], z_s.at[i], z_r.at[i], at_z(step_of(i))).wait_recv()
            xa(i, True).start()
            xa(i, False).start()

        @pl.when((i >= 1) & (i < NZ + 1))
        def _():
            k = i - 1
            n = source_of(k)
            left, right = feat.at[(x + NX - 1) % NX, n], feat.at[(x + 1) % NX, n]
            remote(left, left, xa_s.at[k, 0], xa_r.at[k, 0], at_x(-1)).wait_recv()
            xf(k, True).start()
            remote(right, right, xa_s.at[k, 1], xa_r.at[k, 1], at_x(1)).wait_recv()
            xf(k, False).start()

        @pl.when((i >= 2) & (i < NZ + 2))
        def _():
            k = i - 2
            n = source_of(k)
            far = feat.at[(x + 2) % NX, n]
            low, high = far.at[pl.ds(0, half)], far.at[pl.ds(half, half)]
            remote(low, low, xf_s.at[k, 0], xf_r.at[k, 0], at_x(-1)).wait_recv()
            remote(high, high, xf_s.at[k, 1], xf_r.at[k, 1], at_x(1)).wait_recv()
            both = dot(feat[0, n], wgu[0:width, :])
            for q in range(1, NX):
                both = both + dot(feat[q, n], wgu[q * width:(q + 1) * width, :])
            gate, up = both[:, :hw], both[:, hw:]
            hid[x, n] = (gate / (1.0 + jnp.exp(-gate)) * up).astype(BF16)
            ha(k, True).start()
            ha(k, False).start()

        @pl.when((i >= 3) & (i < NZ + 3))
        def _():
            k = i - 3
            n = source_of(k)
            left, right = hid.at[(x + NX - 1) % NX, n], hid.at[(x + 1) % NX, n]
            remote(left, left, ha_s.at[k, 0], ha_r.at[k, 0], at_x(-1)).wait_recv()
            hf(k, True).start()
            remote(right, right, ha_s.at[k, 1], ha_r.at[k, 1], at_x(1)).wait_recv()
            hf(k, False).start()

        @pl.when(i >= 4)
        def _():
            k = i - 4
            n = source_of(k)
            far = hid.at[(x + 2) % NX, n]
            low, high = far.at[pl.ds(0, half)], far.at[pl.ds(half, half)]
            remote(low, low, hf_s.at[k, 0], hf_r.at[k, 0], at_x(-1)).wait_recv()
            remote(high, high, hf_s.at[k, 1], hf_r.at[k, 1], at_x(1)).wait_recv()
            value = dot(hid[0, n], wd[0:hw, :])
            for q in range(1, NX):
                value = value + dot(hid[q, n], wd[q * hw:(q + 1) * hw, :])

            @pl.when(k == 0)
            def _():
                back[z] = value.astype(BF16)

            @pl.when(k > 0)
            def _():
                oexp[n] = value.astype(BF16)
                zback_copy(k).start()

        return carry

    lax.fori_loop(0, NZ + 4, stage, 0)

    def gather(k, carry):
        n = (z + step_of(k) + NZ) % NZ

        @pl.when(k > 0)
        def _():
            remote(oexp.at[n], back.at[n], b_s.at[k], b_r.at[k], at_z(step_of(k))).wait_recv()

        value = dot_rows(comb_hi[n], back[n]) + dot_rows(comb_lo[n], back[n])

        @pl.when(k == 0)
        def _():
            acc[...] = value

        @pl.when(k > 0)
        def _():
            acc[...] += value

        return carry

    lax.fori_loop(0, NZ, gather, 0)
    for q in range(NY):
        ysend[q] = acc[q * nrow:(q + 1) * nrow, :].astype(BF16)
    yr = []
    for d in (4, 3, 5, 2, 6, 1, 7):
        copy = remote(ysend.at[(y + d) % NY], yin.at[d - 1], yr_s.at[d - 1], yr_r.at[d - 1], at_y(d))
        copy.start()
        yr.append(copy)
    total = proj[...] + acc[pl.ds(pl.multiple_of(y * nrow, nrow), nrow), :]
    for d in range(1, NY):
        remote(ysend.at[0], yin.at[d - 1], yr_s.at[d - 1], yr_r.at[d - 1], at_y(d)).wait_recv()
        total = total + yin[d - 1].astype(F32)

    square = jnp.sum(total * total, axis=1, keepdims=True)
    ss_own[...] = jnp.broadcast_to(square, ss_own.shape)
    ss = []
    for d in range(1, NX):
        copy = remote(ss_own, ss_in.at[d - 1], ss_s.at[d - 1], ss_r.at[d - 1], at_x(d))
        copy.start()
        ss.append(copy)
    for d in range(1, NX):
        remote(ss_own, ss_in.at[d - 1], ss_s.at[d - 1], ss_r.at[d - 1], at_x(d)).wait_recv()
        square = square + ss_in[d - 1][:, 0:1]
    scale = lax.rsqrt(square / full + 1e-06)
    out[...] = (total * scale * gain[...]).astype(BF16)

    for copy in meta_copies + rs_copies + yag + yr + ss:
        copy.wait_send()

    def drain(k, carry):
        for make in (xa, xf, ha, hf):
            make(k, True).wait_send()
            make(k, False).wait_send()

        @pl.when(k > 0)
        def _():
            zsend_copy(k).wait_send()
            zback_copy(k).wait_send()

        return carry

    lax.fori_loop(0, NZ, drain, 0)


def body(attn_out, w_out, residual, routes, gates, w_gate, w_up, w_down, norm_gain):
    nrow, width = attn_out.shape
    full = w_out.shape[1]
    topk = routes.shape[1]
    hw = w_gate.shape[2]
    chunk = NY * PAIR
    req = lax.axis_index("req")
    y, z = req // (NC * NZ), (req // NC) % NZ
    y = jnp.where(req % NC == 1, z, y)
    pad = ((0, 8 - topk), (0, 0))
    tile = jnp.concatenate(
        [jnp.pad(routes.T.astype(F32), pad), jnp.pad(gates.T.astype(F32), pad)], axis=0
    )
    odd = y % 2 == 1
    meta = jnp.concatenate([jnp.where(odd, 0.0, tile), jnp.where(odd, tile, 0.0)], axis=1)
    vmem = pl.BlockSpec(memory_space=pltpu.VMEM)
    anyw = pl.BlockSpec(memory_space=pl.ANY)
    dma = pltpu.SemaphoreType.DMA
    scratch = [
        pltpu.VMEM((width, full), BF16),
        pltpu.VMEM((full, 2 * hw), BF16),
        pltpu.VMEM((NX * hw, width), BF16),
        pltpu.VMEM((NX, nrow, width), BF16),
        pltpu.VMEM((NX, nrow, width), F32),
        pltpu.VMEM((NX - 1, nrow, width), BF16),
        pltpu.VMEM((nrow, width), F32),
        pltpu.VMEM((NY, 16, 2 * nrow), F32),
        pltpu.VMEM((NZ, chunk, NY * nrow), BF16),
        pltpu.VMEM((NZ, chunk, NY * nrow), BF16),
        pltpu.VMEM((NZ, chunk, NY * nrow), BF16),
        pltpu.VMEM((NY, nrow, width), BF16),
        pltpu.VMEM((NZ, chunk, width), BF16),
        pltpu.VMEM((NX, NZ, chunk, width), BF16),
        pltpu.VMEM((NX, NZ, chunk, hw), BF16),
        pltpu.VMEM((NZ, chunk, width), BF16),
        pltpu.VMEM((NZ, chunk, width), BF16),
        pltpu.VMEM((NY * nrow, width), F32),
        pltpu.VMEM((NY, nrow, width), BF16),
        pltpu.VMEM((NY - 1, nrow, width), BF16),
        pltpu.VMEM((nrow, 128), F32),
        pltpu.VMEM((NX - 1, nrow, 128), F32),
        dma((4,)),
        dma((NY - 1,)), dma((NY - 1,)),
        dma((NX - 1,)), dma((NX - 1,)),
        dma((NY - 1,)), dma((NY - 1,)),
        dma((NZ,)), dma((NZ,)),
        dma((NZ, 2)), dma((NZ, 2)),
        dma((NZ, 2)), dma((NZ, 2)),
        dma((NZ, 2)), dma((NZ, 2)),
        dma((NZ, 2)), dma((NZ, 2)),
        dma((NZ,)), dma((NZ,)),
        dma((NY - 1,)), dma((NY - 1,)),
        dma((NX - 1,)), dma((NX - 1,)),
    ]
    return pl.pallas_call(
        kernel,
        out_shape=jax.ShapeDtypeStruct((nrow, width), BF16),
        in_specs=[vmem, anyw, vmem, vmem, anyw, anyw, anyw, vmem],
        out_specs=vmem,
        scratch_shapes=scratch,
        compiler_params=pltpu.CompilerParams(collective_id=0, has_side_effects=True),
    )(attn_out, w_out, residual, meta, w_gate[0], w_up[0], w_down[0], norm_gain[None, :])


def solution(mesh):
    placed = (
        P("req", "tp"),
        P("tp", None),
        P("req", "tp"),
        P("req", None),
        P("req", None),
        P("req", None, "tp"),
        P("req", None, "tp"),
        P("req", None, "tp"),
        P("tp"),
    )
    return jax.shard_map(
        body, mesh=mesh, in_specs=placed, out_specs=P("req", "tp"), check_vma=False
    )
```

```python
import functools

import jax
import jax.numpy as jnp
from jax import lax
from jax.experimental import pallas as pl
from jax.experimental.pallas import tpu as pltpu
from jax.sharding import PartitionSpec as P

NY, NZ, NC, NX = 8, 8, 2, 4
CAP = 6
PAIR = NC * CAP
F32, BF16 = jnp.float32, jnp.bfloat16
MESH = pl.DeviceIdType.MESH


def dot(a, b):
    return jnp.dot(a, b, preferred_element_type=F32)


def dot_rows(a, b):
    return lax.dot_general(a, b, (((0,), (0,)), ((), ())), preferred_element_type=F32)


def kernel(
    attn, w_out, resid, routes, gates, w_gate, w_up, w_down, gain, out,
    wo, wgu, wd, part, part32, rs_in, proj, meta_all, pick, comb_hi, comb_lo,
    rows, zsend, feat, hid, oexp, back, acc, ysend, yin, ss_own, ss_in,
    load_sem, meta_s, meta_r, rs_s, rs_r, yag_s, yag_r, z_s, z_r,
    xa_s, xa_r, xf_s, xf_r, ha_s, ha_r, hf_s, hf_r, b_s, b_r, yr_s, yr_r, ss_s, ss_r,
):
    nrow, width = attn.shape
    full = w_out.shape[1]
    chunk = NY * PAIR
    half = chunk // 2
    hw = w_gate.shape[1]
    req, x = lax.axis_index("req"), lax.axis_index("tp")
    c = req % NC
    pz = (req // NC) % NZ
    py = req // (NC * NZ)
    y = py + c * (pz - py)
    z = pz + c * (py - pz)

    def at_x(d):
        return {"tp": (x + d + NX) % NX}

    def chip(yy, zz):
        return yy * (NZ + c * (1 - NZ)) + zz * (1 + c * (NZ - 1))

    def at_y(d):
        return {"req": chip((y + d + NY) % NY, z) * NC + c}

    def at_z(d):
        return {"req": chip(y, (z + d + NZ) % NZ) * NC + c}

    def remote(src, dst, s, r, dev):
        return pltpu.make_async_remote_copy(
            src_ref=src, dst_ref=dst, send_sem=s, recv_sem=r, device_id=dev, device_id_type=MESH
        )

    barrier = pltpu.get_barrier_semaphore()
    partners = [at_x(d) for d in range(1, NX)]
    partners += [at_y(d) for d in range(1, NY)]
    partners += [at_z(d) for d in range(1, NZ)]
    for dev in partners:
        pl.semaphore_signal(barrier, inc=1, device_id=dev, device_id_type=MESH)

    loads = [
        pltpu.make_async_copy(w_out, wo, load_sem.at[0]),
        pltpu.make_async_copy(w_gate, wgu.at[:, :hw], load_sem.at[1]),
        pltpu.make_async_copy(w_up, wgu.at[:, hw:], load_sem.at[2]),
        pltpu.make_async_copy(w_down, wd, load_sem.at[3]),
    ]
    loads[0].start()

    odd = y % 2 == 1
    nk = routes.shape[0]
    meta_all[y] = jnp.zeros((16, 2 * nrow), F32)
    for first, value in ((0, routes[...].astype(F32)), (8, gates[...])):
        meta_all[y, first:first + nk, 0:nrow] = jnp.where(odd, 0.0, value)
        meta_all[y, first:first + nk, nrow:2 * nrow] = jnp.where(odd, value, 0.0)
    loads[0].wait()
    for load in loads[1:]:
        load.start()
    for q in range(NX):
        value = dot(attn[...], wo[:, q * width:(q + 1) * width])
        part32[q] = value
        part[q] = value.astype(BF16)
    pl.semaphore_wait(barrier, len(partners))

    meta_copies, rs_copies = [], []
    for d in (2, 1, 3):
        copy = remote(part.at[(x + d) % NX], rs_in.at[d - 1], rs_s.at[d - 1], rs_r.at[d - 1], at_x(d))
        copy.start()
        rs_copies.append(copy)
    for d in range(1, NY):
        copy = remote(meta_all.at[y], meta_all.at[y], meta_s.at[d - 1], meta_r.at[d - 1], at_y(d))
        copy.start()
        meta_copies.append(copy)

    own = part32[x] + resid[...].astype(F32)
    for d in range(1, NX):
        remote(part.at[0], rs_in.at[d - 1], rs_s.at[d - 1], rs_r.at[d - 1], at_x(d)).wait_recv()
        own = own + rs_in[d - 1].astype(F32)
    proj[...] = own
    rows[y] = own.astype(BF16)

    yag = []
    for d in (4, 3, 5, 2, 6, 1, 7):
        copy = remote(rows.at[y], rows.at[y], yag_s.at[d - 1], yag_r.at[d - 1], at_y(d))
        copy.start()
        yag.append(copy)
    for d in range(1, NY):
        block = meta_all.at[(y - d + NY) % NY]
        remote(block, block, meta_s.at[d - 1], meta_r.at[d - 1], at_y(d)).wait_recv()
    lanes = 2 * nrow
    place = lax.broadcasted_iota(jnp.int32, (chunk, lanes), 0)
    lane = lax.broadcasted_iota(jnp.int32, (chunk, lanes), 1)
    place_y, place_c, place_p = place // PAIR, (place // CAP) % NC, place % CAP
    before = lax.broadcasted_iota(jnp.int32, (lanes, lanes), 0)
    after = lax.broadcasted_iota(jnp.int32, (lanes, lanes), 1)
    earlier = ((before < after) & (before // nrow == after // nrow)).astype(F32).astype(BF16)

    def plan(zz, carry):
        slot = (chip(y, zz) * NC + place_c).astype(F32)
        for j in range(NY // 2):
            both = meta_all[2 * j] + meta_all[2 * j + 1]
            mine = place_y == 2 * j + lane // nrow
            hit = jnp.zeros((chunk, lanes), F32)
            gate = jnp.zeros((chunk, lanes), F32)
            for k in range(6):
                same = mine & (both[k:k + 1, :] == slot)
                hit = jnp.where(same, 1.0, hit)
                gate = jnp.where(same, both[8 + k:9 + k, :], gate)
            rank = dot(hit.astype(BF16), earlier)
            chosen = (hit > 0.0) & (rank == place_p.astype(F32))
            here = pl.ds(j * lanes, lanes)
            pick[zz, :, here] = jnp.where(chosen, 1.0, 0.0).astype(BF16)
            gate = jnp.where(chosen, gate, 0.0)
            high = gate.astype(BF16)
            comb_hi[zz, :, here] = high
            comb_lo[zz, :, here] = (gate - high.astype(F32)).astype(BF16)
        return carry

    lax.fori_loop(0, NZ, plan, 0)

    for d in (1, 7, 2, 6, 3, 5, 4):
        block = rows.at[(y - d + NY) % NY]
        remote(block, block, yag_s.at[d - 1], yag_r.at[d - 1], at_y(-d)).wait_recv()

    def source_of(k):
        return (z - k + NZ) % NZ

    def xa(k, right):
        block = feat.at[x, source_of(k)]
        i = 0 if right else 1
        return remote(block, block, xa_s.at[k, i], xa_r.at[k, i], at_x(1 if right else -1))

    def xf(k, right):
        n = source_of(k)
        i = 0 if right else 1
        rng = pl.ds(0, half) if right else pl.ds(half, half)
        block = feat.at[(x + NX - 1) % NX if right else (x + 1) % NX, n, rng]
        return remote(block, block, xf_s.at[k, i], xf_r.at[k, i], at_x(1 if right else -1))

    def ha(k, right):
        block = hid.at[x, source_of(k)]
        i = 0 if right else 1
        return remote(block, block, ha_s.at[k, i], ha_r.at[k, i], at_x(1 if right else -1))

    def hf(k, right):
        n = source_of(k)
        i = 0 if right else 1
        rng = pl.ds(0, half) if right else pl.ds(half, half)
        block = hid.at[(x + NX - 1) % NX if right else (x + 1) % NX, n, rng]
        return remote(block, block, hf_s.at[k, i], hf_r.at[k, i], at_x(1 if right else -1))

    def zsend_copy(k):
        n = (z + k + NZ) % NZ
        return remote(zsend.at[n], feat.at[x, z], z_s.at[k], z_r.at[k], at_z(k))

    def zback_copy(k):
        n = source_of(k)
        return remote(oexp.at[n], back.at[z], b_s.at[k], b_r.at[k], at_z(-k))

    all_rows = rows[...].reshape(NY * nrow, width)
    feat[x, z] = dot(pick[z], all_rows).astype(BF16)
    xa(0, True).start()
    xa(0, False).start()

    def scatter(k, carry):
        n = (z + k + NZ) % NZ
        zsend[n] = dot(pick[n], rows[...].reshape(NY * nrow, width)).astype(BF16)
        zsend_copy(k).start()
        return carry

    lax.fori_loop(1, NZ, scatter, 0)
    for load in loads[1:]:
        load.wait()

    def stage(i, carry):
        @pl.when((i >= 1) & (i < NZ))
        def _():
            n = source_of(i)
            remote(zsend.at[n], feat.at[x, n], z_s.at[i], z_r.at[i], at_z(i)).wait_recv()
            xa(i, True).start()
            xa(i, False).start()

        @pl.when((i >= 1) & (i < NZ + 1))
        def _():
            k = i - 1
            n = source_of(k)
            left, right = feat.at[(x + NX - 1) % NX, n], feat.at[(x + 1) % NX, n]
            remote(left, left, xa_s.at[k, 0], xa_r.at[k, 0], at_x(-1)).wait_recv()
            xf(k, True).start()
            remote(right, right, xa_s.at[k, 1], xa_r.at[k, 1], at_x(1)).wait_recv()
            xf(k, False).start()

        @pl.when((i >= 2) & (i < NZ + 2))
        def _():
            k = i - 2
            n = source_of(k)
            far = feat.at[(x + 2) % NX, n]
            low, high = far.at[pl.ds(0, half)], far.at[pl.ds(half, half)]
            remote(low, low, xf_s.at[k, 0], xf_r.at[k, 0], at_x(-1)).wait_recv()
            remote(high, high, xf_s.at[k, 1], xf_r.at[k, 1], at_x(1)).wait_recv()
            both = dot(feat[0, n], wgu[0:width, :])
            for q in range(1, NX):
                both = both + dot(feat[q, n], wgu[q * width:(q + 1) * width, :])
            gate, up = both[:, :hw], both[:, hw:]
            hid[x, n] = (gate / (1.0 + jnp.exp(-gate)) * up).astype(BF16)
            ha(k, True).start()
            ha(k, False).start()

        @pl.when((i >= 3) & (i < NZ + 3))
        def _():
            k = i - 3
            n = source_of(k)
            left, right = hid.at[(x + NX - 1) % NX, n], hid.at[(x + 1) % NX, n]
            remote(left, left, ha_s.at[k, 0], ha_r.at[k, 0], at_x(-1)).wait_recv()
            hf(k, True).start()
            remote(right, right, ha_s.at[k, 1], ha_r.at[k, 1], at_x(1)).wait_recv()
            hf(k, False).start()

        @pl.when((i >= 4) & (i < NZ + 4))
        def _():
            k = i - 4
            n = source_of(k)
            far = hid.at[(x + 2) % NX, n]
            low, high = far.at[pl.ds(0, half)], far.at[pl.ds(half, half)]
            remote(low, low, hf_s.at[k, 0], hf_r.at[k, 0], at_x(-1)).wait_recv()
            remote(high, high, hf_s.at[k, 1], hf_r.at[k, 1], at_x(1)).wait_recv()
            value = dot(hid[0, n], wd[0:hw, :])
            for q in range(1, NX):
                value = value + dot(hid[q, n], wd[q * hw:(q + 1) * hw, :])

            @pl.when(k == 0)
            def _():
                back[z] = value.astype(BF16)

            @pl.when(k > 0)
            def _():
                oexp[n] = value.astype(BF16)
                zback_copy(k).start()

        @pl.when(i >= 6)
        def _():
            k = i - 6
            n = (z + k) % NZ

            @pl.when(k > 0)
            def _():
                remote(oexp.at[n], back.at[n], b_s.at[k], b_r.at[k], at_z(k)).wait_recv()

            acc[...] += dot_rows(comb_hi[n], back[n]) + dot_rows(comb_lo[n], back[n])

        return carry

    acc[...] = jnp.zeros(acc.shape, F32)
    lax.fori_loop(0, NZ + 6, stage, 0)

    for q in range(NY):
        ysend[q] = acc[q * nrow:(q + 1) * nrow, :].astype(BF16)
    yr = []
    for d in (4, 3, 5, 2, 6, 1, 7):
        copy = remote(ysend.at[(y + d) % NY], yin.at[d - 1], yr_s.at[d - 1], yr_r.at[d - 1], at_y(d))
        copy.start()
        yr.append(copy)
    total = proj[...] + acc[pl.ds(pl.multiple_of(y * nrow, nrow), nrow), :]
    for d in range(1, NY):
        remote(ysend.at[0], yin.at[d - 1], yr_s.at[d - 1], yr_r.at[d - 1], at_y(d)).wait_recv()
        total = total + yin[d - 1].astype(F32)

    square = jnp.sum(total * total, axis=1, keepdims=True)
    ss_own[...] = jnp.broadcast_to(square, ss_own.shape)
    ss = []
    for d in range(1, NX):
        copy = remote(ss_own, ss_in.at[d - 1], ss_s.at[d - 1], ss_r.at[d - 1], at_x(d))
        copy.start()
        ss.append(copy)
    for d in range(1, NX):
        remote(ss_own, ss_in.at[d - 1], ss_s.at[d - 1], ss_r.at[d - 1], at_x(d)).wait_recv()
        square = square + ss_in[d - 1][:, 0:1]
    scale = lax.rsqrt(square / full + 1e-06)
    out[...] = (total * scale * gain[...]).astype(BF16)

    for copy in meta_copies + rs_copies + yag + yr + ss:
        copy.wait_send()

    def drain(k, carry):
        for make in (xa, xf, ha, hf):
            make(k, True).wait_send()
            make(k, False).wait_send()

        @pl.when(k > 0)
        def _():
            zsend_copy(k).wait_send()
            zback_copy(k).wait_send()

        return carry

    lax.fori_loop(0, NZ, drain, 0)


def body(attn_out, w_out, residual, routes, gates, w_gate, w_up, w_down, norm_gain):
    nrow, width = attn_out.shape
    full = w_out.shape[1]
    hw = w_gate.shape[2]
    chunk = NY * PAIR
    vmem = pl.BlockSpec(memory_space=pltpu.VMEM)
    anyw = pl.BlockSpec(memory_space=pl.ANY)
    dma = pltpu.SemaphoreType.DMA
    scratch = [
        pltpu.VMEM((width, full), BF16),
        pltpu.VMEM((full, 2 * hw), BF16),
        pltpu.VMEM((NX * hw, width), BF16),
        pltpu.VMEM((NX, nrow, width), BF16),
        pltpu.VMEM((NX, nrow, width), F32),
        pltpu.VMEM((NX - 1, nrow, width), BF16),
        pltpu.VMEM((nrow, width), F32),
        pltpu.VMEM((NY, 16, 2 * nrow), F32),
        pltpu.VMEM((NZ, chunk, NY * nrow), BF16),
        pltpu.VMEM((NZ, chunk, NY * nrow), BF16),
        pltpu.VMEM((NZ, chunk, NY * nrow), BF16),
        pltpu.VMEM((NY, nrow, width), BF16),
        pltpu.VMEM((NZ, chunk, width), BF16),
        pltpu.VMEM((NX, NZ, chunk, width), BF16),
        pltpu.VMEM((NX, NZ, chunk, hw), BF16),
        pltpu.VMEM((NZ, chunk, width), BF16),
        pltpu.VMEM((NZ, chunk, width), BF16),
        pltpu.VMEM((NY * nrow, width), F32),
        pltpu.VMEM((NY, nrow, width), BF16),
        pltpu.VMEM((NY - 1, nrow, width), BF16),
        pltpu.VMEM((nrow, 128), F32),
        pltpu.VMEM((NX - 1, nrow, 128), F32),
        dma((4,)),
        dma((NY - 1,)), dma((NY - 1,)),
        dma((NX - 1,)), dma((NX - 1,)),
        dma((NY - 1,)), dma((NY - 1,)),
        dma((NZ,)), dma((NZ,)),
        dma((NZ, 2)), dma((NZ, 2)),
        dma((NZ, 2)), dma((NZ, 2)),
        dma((NZ, 2)), dma((NZ, 2)),
        dma((NZ, 2)), dma((NZ, 2)),
        dma((NZ,)), dma((NZ,)),
        dma((NY - 1,)), dma((NY - 1,)),
        dma((NX - 1,)), dma((NX - 1,)),
    ]
    return pl.pallas_call(
        kernel,
        out_shape=jax.ShapeDtypeStruct((nrow, width), BF16),
        in_specs=[vmem, anyw, vmem, vmem, vmem, anyw, anyw, anyw, vmem],
        out_specs=vmem,
        scratch_shapes=scratch,
        compiler_params=pltpu.CompilerParams(collective_id=0, has_side_effects=True),
    )(attn_out, w_out, residual, routes.T, gates.T, w_gate[0], w_up[0], w_down[0], norm_gain[None, :])


def solution(mesh):
    placed = (
        P("req", "tp"),
        P("tp", None),
        P("req", "tp"),
        P("req", None),
        P("req", None),
        P("req", None, "tp"),
        P("req", None, "tp"),
        P("req", None, "tp"),
        P("tp"),
    )
    return jax.shard_map(
        body, mesh=mesh, in_specs=placed, out_specs=P("req", "tp"), check_vma=False
    )
```

```python
import functools

import jax
import jax.numpy as jnp
from jax import lax
from jax.experimental import pallas as pl
from jax.experimental.pallas import tpu as pltpu
from jax.sharding import PartitionSpec as P

NY, NZ, NC, NX = 8, 8, 2, 4
CAP = 6
PAIR = NC * CAP
F32, BF16 = jnp.float32, jnp.bfloat16
MESH = pl.DeviceIdType.MESH


def dot(a, b):
    return jnp.dot(a, b, preferred_element_type=F32)


def dot_rows(a, b):
    return lax.dot_general(a, b, (((0,), (0,)), ((), ())), preferred_element_type=F32)


def kernel(
    attn, w_out, resid, routes, gates, w_gate, w_up, w_down, gain, out,
    wo, wgu, wd, part, part32, rs_in, proj, meta_all, pick, comb_hi, comb_lo,
    rows, zsend, feat, hid, oexp, back, acc, ysend, yin, ss_own, ss_in,
    load_sem, meta_s, meta_r, rs_s, rs_r, yag_s, yag_r, z_s, z_r,
    xa_s, xa_r, xf_s, xf_r, ha_s, ha_r, hf_s, hf_r, b_s, b_r, yr_s, yr_r, ss_s, ss_r,
):
    nrow, width = attn.shape
    full = w_out.shape[1]
    chunk = NY * PAIR
    half = chunk // 2
    hw = w_gate.shape[1]
    req, x = lax.axis_index("req"), lax.axis_index("tp")
    c = req % NC
    pz = (req // NC) % NZ
    py = req // (NC * NZ)
    y = py + c * (pz - py)
    z = pz + c * (py - pz)

    def at_x(d):
        return {"tp": (x + d + NX) % NX}

    def chip(yy, zz):
        return yy * (NZ + c * (1 - NZ)) + zz * (1 + c * (NZ - 1))

    def at_y(d):
        return {"req": chip((y + d + NY) % NY, z) * NC + c}

    def at_z(d):
        return {"req": chip(y, (z + d + NZ) % NZ) * NC + c}

    def remote(src, dst, s, r, dev):
        return pltpu.make_async_remote_copy(
            src_ref=src, dst_ref=dst, send_sem=s, recv_sem=r, device_id=dev, device_id_type=MESH
        )

    barrier = pltpu.get_barrier_semaphore()
    partners = [at_x(d) for d in range(1, NX)]
    partners += [at_y(d) for d in range(1, NY)]
    partners += [at_z(d) for d in range(1, NZ)]
    for dev in partners:
        pl.semaphore_signal(barrier, inc=1, device_id=dev, device_id_type=MESH)

    loads = [
        pltpu.make_async_copy(w_out, wo, load_sem.at[0]),
        pltpu.make_async_copy(w_gate, wgu.at[:, :hw], load_sem.at[1]),
        pltpu.make_async_copy(w_up, wgu.at[:, hw:], load_sem.at[2]),
        pltpu.make_async_copy(w_down, wd, load_sem.at[3]),
    ]
    loads[0].start()

    odd = y % 2 == 1
    nk = routes.shape[0]
    meta_all[y] = jnp.zeros((16, 2 * nrow), F32)
    for first, value in ((0, routes[...].astype(F32)), (8, gates[...])):
        meta_all[y, first:first + nk, 0:nrow] = jnp.where(odd, 0.0, value)
        meta_all[y, first:first + nk, nrow:2 * nrow] = jnp.where(odd, value, 0.0)
    loads[0].wait()
    for load in loads[1:]:
        load.start()
    for q in range(NX):
        value = dot(attn[...], wo[:, q * width:(q + 1) * width])
        part32[q] = value
        part[q] = value.astype(BF16)
    pl.semaphore_wait(barrier, len(partners))

    meta_copies, rs_copies = [], []
    for d in (2, 1, 3):
        copy = remote(part.at[(x + d) % NX], rs_in.at[d - 1], rs_s.at[d - 1], rs_r.at[d - 1], at_x(d))
        copy.start()
        rs_copies.append(copy)
    for d in range(1, NY):
        copy = remote(meta_all.at[y], meta_all.at[y], meta_s.at[d - 1], meta_r.at[d - 1], at_y(d))
        copy.start()
        meta_copies.append(copy)

    own = part32[x] + resid[...].astype(F32)
    for d in range(1, NX):
        remote(part.at[0], rs_in.at[d - 1], rs_s.at[d - 1], rs_r.at[d - 1], at_x(d)).wait_recv()
        own = own + rs_in[d - 1].astype(F32)
    proj[...] = own
    rows[y] = own.astype(BF16)

    yag = []
    for d in (4, 3, 5, 2, 6, 1, 7):
        copy = remote(rows.at[y], rows.at[y], yag_s.at[d - 1], yag_r.at[d - 1], at_y(d))
        copy.start()
        yag.append(copy)
    for d in range(1, NY):
        block = meta_all.at[(y - d + NY) % NY]
        remote(block, block, meta_s.at[d - 1], meta_r.at[d - 1], at_y(d)).wait_recv()
    lanes = 2 * nrow
    place = lax.broadcasted_iota(jnp.int32, (chunk, lanes), 0)
    lane = lax.broadcasted_iota(jnp.int32, (chunk, lanes), 1)
    place_y, place_c, place_p = place // PAIR, (place // CAP) % NC, place % CAP
    before = lax.broadcasted_iota(jnp.int32, (lanes, lanes), 0)
    after = lax.broadcasted_iota(jnp.int32, (lanes, lanes), 1)
    earlier = ((before < after) & (before // nrow == after // nrow)).astype(F32).astype(BF16)

    def plan(zz, carry):
        slot = (chip(y, zz) * NC + place_c).astype(F32)
        for j in range(NY // 2):
            both = meta_all[2 * j] + meta_all[2 * j + 1]
            mine = place_y == 2 * j + lane // nrow
            hit = jnp.zeros((chunk, lanes), F32)
            gate = jnp.zeros((chunk, lanes), F32)
            for k in range(6):
                same = mine & (both[k:k + 1, :] == slot)
                hit = jnp.where(same, 1.0, hit)
                gate = jnp.where(same, both[8 + k:9 + k, :], gate)
            rank = dot(hit.astype(BF16), earlier)
            chosen = (hit > 0.0) & (rank == place_p.astype(F32))
            here = pl.ds(j * lanes, lanes)
            pick[zz, :, here] = jnp.where(chosen, 1.0, 0.0).astype(BF16)
            gate = jnp.where(chosen, gate, 0.0)
            high = gate.astype(BF16)
            comb_hi[zz, :, here] = high
            comb_lo[zz, :, here] = (gate - high.astype(F32)).astype(BF16)
        return carry

    lax.fori_loop(0, NZ, plan, 0)

    for d in (1, 7, 2, 6, 3, 5, 4):
        block = rows.at[(y - d + NY) % NY]
        remote(block, block, yag_s.at[d - 1], yag_r.at[d - 1], at_y(-d)).wait_recv()

    def source_of(k):
        return (z - k + NZ) % NZ

    def xa(k, right):
        block = feat.at[x, source_of(k)]
        i = 0 if right else 1
        return remote(block, block, xa_s.at[k, i], xa_r.at[k, i], at_x(1 if right else -1))

    def xf(k, right):
        n = source_of(k)
        i = 0 if right else 1
        rng = pl.ds(0, half) if right else pl.ds(half, half)
        block = feat.at[(x + NX - 1) % NX if right else (x + 1) % NX, n, rng]
        return remote(block, block, xf_s.at[k, i], xf_r.at[k, i], at_x(1 if right else -1))

    def ha(k, right):
        block = hid.at[x, source_of(k)]
        i = 0 if right else 1
        return remote(block, block, ha_s.at[k, i], ha_r.at[k, i], at_x(1 if right else -1))

    def hf(k, right):
        n = source_of(k)
        i = 0 if right else 1
        rng = pl.ds(0, half) if right else pl.ds(half, half)
        block = hid.at[(x + NX - 1) % NX if right else (x + 1) % NX, n, rng]
        return remote(block, block, hf_s.at[k, i], hf_r.at[k, i], at_x(1 if right else -1))

    def zsend_copy(k):
        n = (z + k + NZ) % NZ
        return remote(zsend.at[n], feat.at[x, z], z_s.at[k], z_r.at[k], at_z(k))

    def zback_copy(k):
        n = source_of(k)
        return remote(oexp.at[n], back.at[z], b_s.at[k], b_r.at[k], at_z(-k))

    all_rows = rows[...].reshape(NY * nrow, width)
    feat[x, z] = dot(pick[z], all_rows).astype(BF16)
    xa(0, True).start()
    xa(0, False).start()

    def scatter(k, carry):
        n = (z + k + NZ) % NZ
        zsend[n] = dot(pick[n], rows[...].reshape(NY * nrow, width)).astype(BF16)
        zsend_copy(k).start()
        return carry

    lax.fori_loop(1, NZ, scatter, 0)
    for load in loads[1:]:
        load.wait()

    def stage(i, carry):
        @pl.when((i >= 1) & (i < NZ))
        def _():
            n = source_of(i)
            remote(zsend.at[n], feat.at[x, n], z_s.at[i], z_r.at[i], at_z(i)).wait_recv()
            xa(i, True).start()
            xa(i, False).start()

        @pl.when((i >= 1) & (i < NZ + 1))
        def _():
            k = i - 1
            n = source_of(k)
            left, right = feat.at[(x + NX - 1) % NX, n], feat.at[(x + 1) % NX, n]
            remote(left, left, xa_s.at[k, 0], xa_r.at[k, 0], at_x(-1)).wait_recv()
            xf(k, True).start()
            remote(right, right, xa_s.at[k, 1], xa_r.at[k, 1], at_x(1)).wait_recv()
            xf(k, False).start()

        @pl.when((i >= 2) & (i < NZ + 2))
        def _():
            k = i - 2
            n = source_of(k)
            far = feat.at[(x + 2) % NX, n]
            low, high = far.at[pl.ds(0, half)], far.at[pl.ds(half, half)]
            remote(low, low, xf_s.at[k, 0], xf_r.at[k, 0], at_x(-1)).wait_recv()
            remote(high, high, xf_s.at[k, 1], xf_r.at[k, 1], at_x(1)).wait_recv()
            both = dot(feat[0, n], wgu[0:width, :])
            for q in range(1, NX):
                both = both + dot(feat[q, n], wgu[q * width:(q + 1) * width, :])
            gate, up = both[:, :hw], both[:, hw:]
            hid[x, n] = (gate / (1.0 + jnp.exp(-gate)) * up).astype(BF16)

        @pl.when((i >= 5) & (i < NZ + 2))
        def _():
            ha(i - 5, True).start()
            ha(i - 5, False).start()

        @pl.when(i == NZ + 1)
        def _():
            for k in range(NZ - 3, NZ):
                ha(k, True).start()
                ha(k, False).start()

        @pl.when((i >= 6) & (i < NZ + 6))
        def _():
            k = i - 6
            n = source_of(k)
            left, right = hid.at[(x + NX - 1) % NX, n], hid.at[(x + 1) % NX, n]
            remote(left, left, ha_s.at[k, 0], ha_r.at[k, 0], at_x(-1)).wait_recv()
            hf(k, True).start()
            remote(right, right, ha_s.at[k, 1], ha_r.at[k, 1], at_x(1)).wait_recv()
            hf(k, False).start()

        @pl.when((i >= 7) & (i < NZ + 7))
        def _():
            k = i - 7
            n = source_of(k)
            far = hid.at[(x + 2) % NX, n]
            low, high = far.at[pl.ds(0, half)], far.at[pl.ds(half, half)]
            remote(low, low, hf_s.at[k, 0], hf_r.at[k, 0], at_x(-1)).wait_recv()
            remote(high, high, hf_s.at[k, 1], hf_r.at[k, 1], at_x(1)).wait_recv()
            value = dot(hid[0, n], wd[0:hw, :])
            for q in range(1, NX):
                value = value + dot(hid[q, n], wd[q * hw:(q + 1) * hw, :])

            @pl.when(k == 0)
            def _():
                back[z] = value.astype(BF16)

            @pl.when(k > 0)
            def _():
                oexp[n] = value.astype(BF16)
                zback_copy(k).start()

        @pl.when(i >= 9)
        def _():
            k = i - 9
            n = (z + k) % NZ

            @pl.when(k > 0)
            def _():
                remote(oexp.at[n], back.at[n], b_s.at[k], b_r.at[k], at_z(k)).wait_recv()

            acc[...] += dot_rows(comb_hi[n], back[n]) + dot_rows(comb_lo[n], back[n])

        return carry

    acc[...] = jnp.zeros(acc.shape, F32)
    lax.fori_loop(0, NZ + 9, stage, 0)

    for q in range(NY):
        ysend[q] = acc[q * nrow:(q + 1) * nrow, :].astype(BF16)
    yr = []
    for d in (4, 3, 5, 2, 6, 1, 7):
        copy = remote(ysend.at[(y + d) % NY], yin.at[d - 1], yr_s.at[d - 1], yr_r.at[d - 1], at_y(d))
        copy.start()
        yr.append(copy)
    total = proj[...] + acc[pl.ds(pl.multiple_of(y * nrow, nrow), nrow), :]
    for d in range(1, NY):
        remote(ysend.at[0], yin.at[d - 1], yr_s.at[d - 1], yr_r.at[d - 1], at_y(d)).wait_recv()
        total = total + yin[d - 1].astype(F32)

    square = jnp.sum(total * total, axis=1, keepdims=True)
    ss_own[...] = jnp.broadcast_to(square, ss_own.shape)
    ss = []
    for d in range(1, NX):
        copy = remote(ss_own, ss_in.at[d - 1], ss_s.at[d - 1], ss_r.at[d - 1], at_x(d))
        copy.start()
        ss.append(copy)
    for d in range(1, NX):
        remote(ss_own, ss_in.at[d - 1], ss_s.at[d - 1], ss_r.at[d - 1], at_x(d)).wait_recv()
        square = square + ss_in[d - 1][:, 0:1]
    scale = lax.rsqrt(square / full + 1e-06)
    out[...] = (total * scale * gain[...]).astype(BF16)

    for copy in meta_copies + rs_copies + yag + yr + ss:
        copy.wait_send()

    def drain(k, carry):
        for make in (xa, xf, ha, hf):
            make(k, True).wait_send()
            make(k, False).wait_send()

        @pl.when(k > 0)
        def _():
            zsend_copy(k).wait_send()
            zback_copy(k).wait_send()

        return carry

    lax.fori_loop(0, NZ, drain, 0)


def body(attn_out, w_out, residual, routes, gates, w_gate, w_up, w_down, norm_gain):
    nrow, width = attn_out.shape
    full = w_out.shape[1]
    hw = w_gate.shape[2]
    chunk = NY * PAIR
    vmem = pl.BlockSpec(memory_space=pltpu.VMEM)
    anyw = pl.BlockSpec(memory_space=pl.ANY)
    dma = pltpu.SemaphoreType.DMA
    scratch = [
        pltpu.VMEM((width, full), BF16),
        pltpu.VMEM((full, 2 * hw), BF16),
        pltpu.VMEM((NX * hw, width), BF16),
        pltpu.VMEM((NX, nrow, width), BF16),
        pltpu.VMEM((NX, nrow, width), F32),
        pltpu.VMEM((NX - 1, nrow, width), BF16),
        pltpu.VMEM((nrow, width), F32),
        pltpu.VMEM((NY, 16, 2 * nrow), F32),
        pltpu.VMEM((NZ, chunk, NY * nrow), BF16),
        pltpu.VMEM((NZ, chunk, NY * nrow), BF16),
        pltpu.VMEM((NZ, chunk, NY * nrow), BF16),
        pltpu.VMEM((NY, nrow, width), BF16),
        pltpu.VMEM((NZ, chunk, width), BF16),
        pltpu.VMEM((NX, NZ, chunk, width), BF16),
        pltpu.VMEM((NX, NZ, chunk, hw), BF16),
        pltpu.VMEM((NZ, chunk, width), BF16),
        pltpu.VMEM((NZ, chunk, width), BF16),
        pltpu.VMEM((NY * nrow, width), F32),
        pltpu.VMEM((NY, nrow, width), BF16),
        pltpu.VMEM((NY - 1, nrow, width), BF16),
        pltpu.VMEM((nrow, 128), F32),
        pltpu.VMEM((NX - 1, nrow, 128), F32),
        dma((4,)),
        dma((NY - 1,)), dma((NY - 1,)),
        dma((NX - 1,)), dma((NX - 1,)),
        dma((NY - 1,)), dma((NY - 1,)),
        dma((NZ,)), dma((NZ,)),
        dma((NZ, 2)), dma((NZ, 2)),
        dma((NZ, 2)), dma((NZ, 2)),
        dma((NZ, 2)), dma((NZ, 2)),
        dma((NZ, 2)), dma((NZ, 2)),
        dma((NZ,)), dma((NZ,)),
        dma((NY - 1,)), dma((NY - 1,)),
        dma((NX - 1,)), dma((NX - 1,)),
    ]
    return pl.pallas_call(
        kernel,
        out_shape=jax.ShapeDtypeStruct((nrow, width), BF16),
        in_specs=[vmem, anyw, vmem, vmem, vmem, anyw, anyw, anyw, vmem],
        out_specs=vmem,
        scratch_shapes=scratch,
        compiler_params=pltpu.CompilerParams(collective_id=0, has_side_effects=True),
    )(attn_out, w_out, residual, routes.T, gates.T, w_gate[0], w_up[0], w_down[0], norm_gain[None, :])


def solution(mesh):
    placed = (
        P("req", "tp"),
        P("tp", None),
        P("req", "tp"),
        P("req", None),
        P("req", None),
        P("req", None, "tp"),
        P("req", None, "tp"),
        P("req", None, "tp"),
        P("tp"),
    )
    return jax.shard_map(
        body, mesh=mesh, in_specs=placed, out_specs=P("req", "tp"), check_vma=False
    )
```

```python
import functools

import jax
import jax.numpy as jnp
from jax import lax
from jax.experimental import pallas as pl
from jax.experimental.pallas import tpu as pltpu
from jax.sharding import PartitionSpec as P

NY, NZ, NC, NX = 8, 8, 2, 4
CAP = 6
PAIR = NC * CAP
TILE = 16
F32, BF16 = jnp.float32, jnp.bfloat16
MESH = pl.DeviceIdType.MESH


def dot(a, b):
    return jnp.dot(a, b, preferred_element_type=F32)


def dot_rows(a, b):
    return lax.dot_general(a, b, (((0,), (0,)), ((), ())), preferred_element_type=F32)


def kernel(
    attn, w_out, resid, routes, gates, w_gate, w_up, w_down, gain, out,
    wo, wgu, wd, part, part32, rs_in, proj, meta_all, pick, comb_hi, comb_lo, spread,
    rows, zsend, feat, hid, oexp, back, acc, ysend, yin, ss_own, ss_in,
    load_sem, meta_s, meta_r, rs_s, rs_r, yag_s, yag_r, z_s, z_r,
    xa_s, xa_r, xf_s, xf_r, ha_s, ha_r, hf_s, hf_r, b_s, b_r, yr_s, yr_r, ss_s, ss_r,
):
    nrow, width = attn.shape
    full = w_out.shape[1]
    chunk = NY * PAIR
    half = chunk // 2
    hw = w_gate.shape[1]
    req, x = lax.axis_index("req"), lax.axis_index("tp")
    c = req % NC
    pz = (req // NC) % NZ
    py = req // (NC * NZ)
    y = py + c * (pz - py)
    z = pz + c * (py - pz)

    def at_x(d):
        return {"tp": (x + d + NX) % NX}

    def chip(yy, zz):
        return yy * (NZ + c * (1 - NZ)) + zz * (1 + c * (NZ - 1))

    def at_y(d):
        return {"req": chip((y + d + NY) % NY, z) * NC + c}

    def at_z(d):
        return {"req": chip(y, (z + d + NZ) % NZ) * NC + c}

    def remote(src, dst, s, r, dev):
        return pltpu.make_async_remote_copy(
            src_ref=src, dst_ref=dst, send_sem=s, recv_sem=r, device_id=dev, device_id_type=MESH
        )

    barrier = pltpu.get_barrier_semaphore()
    partners = [at_x(d) for d in range(1, NX)]
    partners += [at_y(d) for d in range(1, NY)]
    partners += [at_z(d) for d in range(1, NZ)]
    for dev in partners:
        pl.semaphore_signal(barrier, inc=1, device_id=dev, device_id_type=MESH)

    loads = [
        pltpu.make_async_copy(w_out, wo, load_sem.at[0]),
        pltpu.make_async_copy(w_gate, wgu.at[:, :hw], load_sem.at[1]),
        pltpu.make_async_copy(w_up, wgu.at[:, hw:], load_sem.at[2]),
        pltpu.make_async_copy(w_down, wd, load_sem.at[3]),
    ]
    loads[0].start()

    odd = y % 2 == 1
    nk = routes.shape[0]
    meta_all[y] = jnp.zeros((16, 2 * nrow), F32)
    for first, value in ((0, routes[...].astype(F32)), (8, gates[...])):
        meta_all[y, first:first + nk, 0:nrow] = jnp.where(odd, 0.0, value)
        meta_all[y, first:first + nk, nrow:2 * nrow] = jnp.where(odd, value, 0.0)
    loads[0].wait()
    for load in loads[1:]:
        load.start()
    for q in range(NX):
        value = dot(attn[...], wo[:, q * width:(q + 1) * width])
        part32[q] = value
        part[q] = value.astype(BF16)
    pl.semaphore_wait(barrier, len(partners))

    meta_copies, rs_copies = [], []
    for d in (2, 1, 3):
        copy = remote(part.at[(x + d) % NX], rs_in.at[d - 1], rs_s.at[d - 1], rs_r.at[d - 1], at_x(d))
        copy.start()
        rs_copies.append(copy)
    for d in range(1, NY):
        copy = remote(meta_all.at[y], meta_all.at[y], meta_s.at[d - 1], meta_r.at[d - 1], at_y(d))
        copy.start()
        meta_copies.append(copy)

    own = part32[x] + resid[...].astype(F32)
    for d in range(1, NX):
        remote(part.at[0], rs_in.at[d - 1], rs_s.at[d - 1], rs_r.at[d - 1], at_x(d)).wait_recv()
        own = own + rs_in[d - 1].astype(F32)
    proj[...] = own
    rows[y] = own.astype(BF16)

    yag = []
    for d in (4, 3, 5, 2, 6, 1, 7):
        copy = remote(rows.at[y], rows.at[y], yag_s.at[d - 1], yag_r.at[d - 1], at_y(d))
        copy.start()
        yag.append(copy)
    for d in range(1, NY):
        block = meta_all.at[(y - d + NY) % NY]
        remote(block, block, meta_s.at[d - 1], meta_r.at[d - 1], at_y(d)).wait_recv()
    lanes = 2 * nrow
    place = lax.broadcasted_iota(jnp.int32, (chunk, lanes), 0)
    lane = lax.broadcasted_iota(jnp.int32, (chunk, lanes), 1)
    place_y, place_c, place_p = place // PAIR, (place // CAP) % NC, place % CAP
    before = lax.broadcasted_iota(jnp.int32, (lanes, lanes), 0)
    after = lax.broadcasted_iota(jnp.int32, (lanes, lanes), 1)
    earlier = ((before < after) & (before // nrow == after // nrow)).astype(F32).astype(BF16)

    def plan(zz, carry):
        slot = (chip(y, zz) * NC + place_c).astype(F32)
        for j in range(NY // 2):
            both = meta_all[2 * j] + meta_all[2 * j + 1]
            mine = place_y == 2 * j + lane // nrow
            hit = jnp.zeros((chunk, lanes), F32)
            for k in range(nk):
                hit = jnp.where(both[k:k + 1, :] == slot, 1.0, hit)
            hit = jnp.where(mine, hit, 0.0)
            rank = dot(hit.astype(BF16), earlier)
            chosen = (hit > 0.0) & (rank == place_p.astype(F32))
            here = pl.ds(j * lanes, lanes)
            pick[zz, :, here] = jnp.where(chosen, 1.0, 0.0).astype(BF16)
        return carry

    lax.fori_loop(0, NZ, plan, 0)

    line = lax.broadcasted_iota(jnp.int32, (NY * TILE, lanes), 0)
    in_y, in_q = line // TILE, line % TILE
    mine_home = (lax.broadcasted_iota(jnp.int32, line.shape, 1) // nrow == y % 2) & (in_q < PAIR)

    def plan_home(zz, carry):
        slot = (chip(in_y, zz) * NC + in_q // CAP).astype(F32)
        own = meta_all[y]
        hit = jnp.zeros(line.shape, F32)
        gate = jnp.zeros(line.shape, F32)
        for k in range(nk):
            same = own[k:k + 1, :] == slot
            hit = jnp.where(same, 1.0, hit)
            gate = jnp.where(same, own[8 + k:9 + k, :], gate)
        hit = jnp.where(mine_home, hit, 0.0)
        rank = dot(hit.astype(BF16), earlier)
        chosen = (hit > 0.0) & (rank == (in_q % CAP).astype(F32))
        gate = jnp.where(chosen, gate, 0.0)
        high = gate.astype(BF16)
        comb_hi[zz] = high
        comb_lo[zz] = (gate - high.astype(F32)).astype(BF16)
        return carry

    lax.fori_loop(0, NZ, plan_home, 0)
    to = lax.broadcasted_iota(jnp.int32, spread.shape, 0)
    of = lax.broadcasted_iota(jnp.int32, spread.shape, 1)
    moved = (to // TILE == of // PAIR) & (to % TILE == of % PAIR)
    spread[...] = jnp.where(moved, 1.0, 0.0).astype(BF16)
    acc[...] = jnp.zeros(acc.shape, F32)

    for d in (1, 7, 2, 6, 3, 5, 4):
        block = rows.at[(y - d + NY) % NY]
        remote(block, block, yag_s.at[d - 1], yag_r.at[d - 1], at_y(-d)).wait_recv()

    def source_of(k):
        return (z - k + NZ) % NZ

    def xa(k, right):
        block = feat.at[x, source_of(k)]
        i = 0 if right else 1
        return remote(block, block, xa_s.at[k, i], xa_r.at[k, i], at_x(1 if right else -1))

    def xf(k, right):
        n = source_of(k)
        i = 0 if right else 1
        rng = pl.ds(0, half) if right else pl.ds(half, half)
        block = feat.at[(x + NX - 1) % NX if right else (x + 1) % NX, n, rng]
        return remote(block, block, xf_s.at[k, i], xf_r.at[k, i], at_x(1 if right else -1))

    def ha(k, right):
        block = hid.at[x, source_of(k)]
        i = 0 if right else 1
        return remote(block, block, ha_s.at[k, i], ha_r.at[k, i], at_x(1 if right else -1))

    def hf(k, right):
        n = source_of(k)
        i = 0 if right else 1
        rng = pl.ds(0, half) if right else pl.ds(half, half)
        block = hid.at[(x + NX - 1) % NX if right else (x + 1) % NX, n, rng]
        return remote(block, block, hf_s.at[k, i], hf_r.at[k, i], at_x(1 if right else -1))

    def zsend_copy(k):
        n = (z + k + NZ) % NZ
        return remote(zsend.at[n], feat.at[x, z], z_s.at[k], z_r.at[k], at_z(k))

    def yr(k, d):
        n = (z + k) % NZ
        return remote(ysend.at[n, (y + d) % NY], yin.at[n, y], yr_s.at[k, d - 1], yr_r.at[k, d - 1], at_y(d))

    def zback_copy(k):
        n = source_of(k)
        return remote(oexp.at[n], back.at[z], b_s.at[k], b_r.at[k], at_z(-k))

    all_rows = rows[...].reshape(NY * nrow, width)
    feat[x, z] = dot(pick[z], all_rows).astype(BF16)
    xa(0, True).start()
    xa(0, False).start()

    def scatter(k, carry):
        n = (z + k + NZ) % NZ
        zsend[n] = dot(pick[n], rows[...].reshape(NY * nrow, width)).astype(BF16)
        zsend_copy(k).start()
        return carry

    lax.fori_loop(1, NZ, scatter, 0)
    for load in loads[1:]:
        load.wait()

    def stage(i, carry):
        @pl.when((i >= 1) & (i < NZ))
        def _():
            n = source_of(i)
            remote(zsend.at[n], feat.at[x, n], z_s.at[i], z_r.at[i], at_z(i)).wait_recv()
            xa(i, True).start()
            xa(i, False).start()

        @pl.when((i >= 1) & (i < NZ + 1))
        def _():
            k = i - 1
            n = source_of(k)
            left, right = feat.at[(x + NX - 1) % NX, n], feat.at[(x + 1) % NX, n]
            remote(left, left, xa_s.at[k, 0], xa_r.at[k, 0], at_x(-1)).wait_recv()
            xf(k, True).start()
            remote(right, right, xa_s.at[k, 1], xa_r.at[k, 1], at_x(1)).wait_recv()
            xf(k, False).start()

        @pl.when((i >= 2) & (i < NZ + 2))
        def _():
            k = i - 2
            n = source_of(k)
            far = feat.at[(x + 2) % NX, n]
            low, high = far.at[pl.ds(0, half)], far.at[pl.ds(half, half)]
            remote(low, low, xf_s.at[k, 0], xf_r.at[k, 0], at_x(-1)).wait_recv()
            remote(high, high, xf_s.at[k, 1], xf_r.at[k, 1], at_x(1)).wait_recv()
            both = dot(feat[0, n], wgu[0:width, :])
            for q in range(1, NX):
                both = both + dot(feat[q, n], wgu[q * width:(q + 1) * width, :])
            gate, up = both[:, :hw], both[:, hw:]
            hid[x, n] = (gate / (1.0 + jnp.exp(-gate)) * up).astype(BF16)
            ha(k, True).start()
            ha(k, False).start()

        @pl.when((i >= 3) & (i < NZ + 3))
        def _():
            k = i - 3
            n = source_of(k)
            left, right = hid.at[(x + NX - 1) % NX, n], hid.at[(x + 1) % NX, n]
            remote(left, left, ha_s.at[k, 0], ha_r.at[k, 0], at_x(-1)).wait_recv()
            hf(k, True).start()
            remote(right, right, ha_s.at[k, 1], ha_r.at[k, 1], at_x(1)).wait_recv()
            hf(k, False).start()

        @pl.when((i >= 4) & (i < NZ + 4))
        def _():
            k = i - 4
            n = source_of(k)
            far = hid.at[(x + 2) % NX, n]
            low, high = far.at[pl.ds(0, half)], far.at[pl.ds(half, half)]
            remote(low, low, hf_s.at[k, 0], hf_r.at[k, 0], at_x(-1)).wait_recv()
            remote(high, high, hf_s.at[k, 1], hf_r.at[k, 1], at_x(1)).wait_recv()
            value = dot(hid[0, n], wd[0:hw, :])
            for q in range(1, NX):
                value = value + dot(hid[q, n], wd[q * hw:(q + 1) * hw, :])

            @pl.when(k == 0)
            def _():
                back[z] = value.astype(BF16)

            @pl.when(k > 0)
            def _():
                oexp[n] = value.astype(BF16)
                zback_copy(k).start()

        @pl.when((i >= 6) & (i < NZ + 6))
        def _():
            k = i - 6
            n = (z + k) % NZ

            @pl.when(k > 0)
            def _():
                remote(oexp.at[n], back.at[n], b_s.at[k], b_r.at[k], at_z(k)).wait_recv()

            value = dot(spread[...], back[n]).astype(BF16)
            ysend[n] = value.reshape(NY, TILE, width)

            def send(d, inner):
                yr(k, d).start()
                return inner

            lax.fori_loop(1, NY, send, 0)
            yin[n, y] = ysend[n, y]

        @pl.when(i >= 8)
        def _():
            k = i - 8
            n = (z + k) % NZ

            def arrive(d, inner):
                block = yin.at[n, (y - d + NY) % NY]
                remote(block, block, yr_s.at[k, d - 1], yr_r.at[k, d - 1], at_y(-d)).wait_recv()
                return inner

            lax.fori_loop(1, NY, arrive, 0)
            value = yin[n].reshape(NY * TILE, width)
            acc[...] += dot_rows(comb_hi[n], value) + dot_rows(comb_lo[n], value)

        return carry

    lax.fori_loop(0, NZ + 8, stage, 0)

    total = proj[...] + acc[pl.ds(pl.multiple_of(y % 2 * nrow, nrow), nrow), :]

    square = jnp.sum(total * total, axis=1, keepdims=True)
    ss_own[...] = jnp.broadcast_to(square, ss_own.shape)
    ss = []
    for d in range(1, NX):
        copy = remote(ss_own, ss_in.at[d - 1], ss_s.at[d - 1], ss_r.at[d - 1], at_x(d))
        copy.start()
        ss.append(copy)
    for d in range(1, NX):
        remote(ss_own, ss_in.at[d - 1], ss_s.at[d - 1], ss_r.at[d - 1], at_x(d)).wait_recv()
        square = square + ss_in[d - 1][:, 0:1]
    scale = lax.rsqrt(square / full + 1e-06)
    out[...] = (total * scale * gain[...]).astype(BF16)

    for copy in meta_copies + rs_copies + yag + ss:
        copy.wait_send()

    def drain(k, carry):
        for make in (xa, xf, ha, hf):
            make(k, True).wait_send()
            make(k, False).wait_send()

        @pl.when(k > 0)
        def _():
            zsend_copy(k).wait_send()
            zback_copy(k).wait_send()

        def sent(d, inner):
            yr(k, d).wait_send()
            return inner

        return lax.fori_loop(1, NY, sent, carry)

    lax.fori_loop(0, NZ, drain, 0)


def body(attn_out, w_out, residual, routes, gates, w_gate, w_up, w_down, norm_gain):
    nrow, width = attn_out.shape
    full = w_out.shape[1]
    hw = w_gate.shape[2]
    chunk = NY * PAIR
    vmem = pl.BlockSpec(memory_space=pltpu.VMEM)
    anyw = pl.BlockSpec(memory_space=pl.ANY)
    dma = pltpu.SemaphoreType.DMA
    scratch = [
        pltpu.VMEM((width, full), BF16),
        pltpu.VMEM((full, 2 * hw), BF16),
        pltpu.VMEM((NX * hw, width), BF16),
        pltpu.VMEM((NX, nrow, width), BF16),
        pltpu.VMEM((NX, nrow, width), F32),
        pltpu.VMEM((NX - 1, nrow, width), BF16),
        pltpu.VMEM((nrow, width), F32),
        pltpu.VMEM((NY, 16, 2 * nrow), F32),
        pltpu.VMEM((NZ, chunk, NY * nrow), BF16),
        pltpu.VMEM((NZ, NY * TILE, 2 * nrow), BF16),
        pltpu.VMEM((NZ, NY * TILE, 2 * nrow), BF16),
        pltpu.VMEM((NY * TILE, chunk), BF16),
        pltpu.VMEM((NY, nrow, width), BF16),
        pltpu.VMEM((NZ, chunk, width), BF16),
        pltpu.VMEM((NX, NZ, chunk, width), BF16),
        pltpu.VMEM((NX, NZ, chunk, hw), BF16),
        pltpu.VMEM((NZ, chunk, width), BF16),
        pltpu.VMEM((NZ, chunk, width), BF16),
        pltpu.VMEM((2 * nrow, width), F32),
        pltpu.VMEM((NZ, NY, TILE, width), BF16),
        pltpu.VMEM((NZ, NY, TILE, width), BF16),
        pltpu.VMEM((nrow, 128), F32),
        pltpu.VMEM((NX - 1, nrow, 128), F32),
        dma((4,)),
        dma((NY - 1,)), dma((NY - 1,)),
        dma((NX - 1,)), dma((NX - 1,)),
        dma((NY - 1,)), dma((NY - 1,)),
        dma((NZ,)), dma((NZ,)),
        dma((NZ, 2)), dma((NZ, 2)),
        dma((NZ, 2)), dma((NZ, 2)),
        dma((NZ, 2)), dma((NZ, 2)),
        dma((NZ, 2)), dma((NZ, 2)),
        dma((NZ,)), dma((NZ,)),
        dma((NZ, NY - 1)), dma((NZ, NY - 1)),
        dma((NX - 1,)), dma((NX - 1,)),
    ]
    return pl.pallas_call(
        kernel,
        out_shape=jax.ShapeDtypeStruct((nrow, width), BF16),
        in_specs=[vmem, anyw, vmem, vmem, vmem, anyw, anyw, anyw, vmem],
        out_specs=vmem,
        scratch_shapes=scratch,
        compiler_params=pltpu.CompilerParams(collective_id=0, has_side_effects=True),
    )(attn_out, w_out, residual, routes.T, gates.T, w_gate[0], w_up[0], w_down[0], norm_gain[None, :])


def solution(mesh):
    placed = (
        P("req", "tp"),
        P("tp", None),
        P("req", "tp"),
        P("req", None),
        P("req", None),
        P("req", None, "tp"),
        P("req", None, "tp"),
        P("req", None, "tp"),
        P("tp"),
    )
    return jax.shard_map(
        body, mesh=mesh, in_specs=placed, out_specs=P("req", "tp"), check_vma=False
    )
```
